512 devices in a mesh: pipe: 16 (over x, y), expert: 32 (over z, core).
Axes of the slice: x: 4, y: 4, z: 16, core: 2. Of those that a mesh axis runs over, the one named last changes fastest.
Arguments:
- fwd_state: bfloat16 [16, 2048, 3584], P('pipe', 'expert'), may hold values from -6 to 6
- rev_state: bfloat16 [16, 2048, 3584], P('pipe', 'expert'), may hold values from -6 to 6
- norm_gain: float32 [16, 3584], P('pipe'), may hold values from 0.5 to 1.5
- w_gate: bfloat16 [16, 3584, 4096], P('pipe', None, 'expert'), may hold values from -0.09375 to 0.09375
- w_up: bfloat16 [16, 3584, 4096], P('pipe', None, 'expert'), may hold values from -0.09375 to 0.09375
- w_down: bfloat16 [16, 4096, 3584], P('pipe', 'expert'), may hold values from -0.1875 to 0.1875
- routes_fwd: int32 [3, 16, 2048, 8], P(None, 'pipe', 'expert'), may hold values from 0 to 255, as said below
- scores_fwd: float32 [3, 16, 2048, 8], P(None, 'pipe', 'expert'), may hold values from 0.02 to 1
- routes_rev: int32 [3, 16, 2048, 8], P(None, 'pipe', 'expert'), may hold values from 0 to 255, as said below
- scores_rev: float32 [3, 16, 2048, 8], P(None, 'pipe', 'expert'), may hold values from 0.02 to 1
Outputs:
- fwd_out: bfloat16 [16, 2048, 3584], P('pipe', 'expert')
- rev_out: bfloat16 [16, 2048, 3584], P('pipe', 'expert')
The draws below stay inside these ranges and needn't reach their ends.
Inputs may be any that keep to these rules, and one draw needn't show every extreme that they name: `routes_fwd`: each row names 8 different experts, all from at most 4 of the 8 groups of 32 consecutive experts. Among the 64 rows of one device, each expert below 4 is named by 1 to 4 rows, and one of them by exactly 4. `routes_rev`: as for routes_fwd.
All inputs are finite; a program needn't handle non-finite values.
Results may differ from the reference program's by a relative error of at most 0.003.
Values may be sent and summed in bfloat16 or wider, within the bound.
No kernel may reach another device: no remote copies, remote signals or barrier semaphores. Data moves between devices by JAX's collectives and lax.ppermute only.
A program may use at most 64 MiB of HBM per device.

```python
import functools
import math
import jax
import jax.numpy as jnp
from jax import lax

D = 3584
MOE_FF = 1024
N_ALL = 256
GROUPS = 8
TOPG = 4
TOPK = 8
SPLIT = 8
CAP = 4
STEPS = 3
TOK_DEV = 64
TOKENS = 2048
HID_DEV = 128
E_FLY = 4
N_PIPE = 16
N_EXPERT = 32


def block_routes(key):
    key_list = jax.random.split(key, 5)
    busiest = jax.random.randint(key_list[0], (), 0, E_FLY)
    counts = jax.random.randint(key_list[1], (E_FLY,), 1, CAP // 2 + 1)
    counts = jnp.where(jnp.arange(E_FLY) == busiest, CAP, counts)
    row_draw = jax.random.randint(key_list[2], (E_FLY, TOK_DEV), 0, 1 << 20)
    row_score = row_draw * TOK_DEV + jnp.arange(TOK_DEV, dtype=jnp.int32)[None, :]
    row_rank = jnp.argsort(jnp.argsort(row_score, axis=1), axis=1)
    hit_mask = row_rank < counts[:, None]
    any_hit = jnp.any(hit_mask, axis=0)
    group_ids = jnp.arange(GROUPS, dtype=jnp.int32)
    group_score = jax.random.randint(key_list[3], (TOK_DEV, GROUPS), 0, 1 << 20) * GROUPS + group_ids[None, :]
    group_score = group_score + jnp.where(any_hit[:, None] & (group_ids[None, :] == 0), 1 << 26, 0)
    group_rank = jnp.argsort(jnp.argsort(-group_score, axis=1), axis=1)
    chosen = group_rank < TOPG
    in_group = jnp.repeat(chosen, N_ALL // GROUPS, axis=1)
    expert_ids = jnp.arange(N_ALL, dtype=jnp.int32)
    base_score = jax.random.randint(key_list[4], (TOK_DEV, N_ALL), 0, 1 << 20) * N_ALL + expert_ids[None, :]
    hit_full = jnp.concatenate([hit_mask.T, jnp.zeros((TOK_DEV, N_ALL - E_FLY), dtype=bool)], axis=1)
    is_flying = expert_ids[None, :] < E_FLY
    final_score = jnp.where(is_flying, jnp.where(hit_full, (1 << 29) + expert_ids[None, :], -1), jnp.where(in_group, base_score, -1))
    picks = jnp.argsort(-final_score, axis=1)[:, :TOPK]
    return picks.astype(jnp.int32)


def all_routes(key, salt):
    key_list = jax.random.split(jax.random.fold_in(key, salt), STEPS * N_PIPE * N_EXPERT)
    drawn = jax.vmap(block_routes)(key_list)
    return drawn.reshape(STEPS, N_PIPE, N_EXPERT * TOK_DEV, TOPK)


def draw_routes_fwd(key, part):
    return all_routes(key, 11)


def draw_routes_rev(key, part):
    return all_routes(key, 23)


def levels(own_key, dims, cuts, least, high):
    def one(position, shards_of):
        steps = jax.random.uniform(jax.random.fold_in(jax.random.fold_in(own_key, 6), position), (shards_of,), jnp.float32, least / len(cuts), high / len(cuts))
        return jnp.repeat(jnp.exp(steps), dims[position] // shards_of).reshape((-1,) + (1,) * (len(dims) - position - 1))

    loudness = one(*cuts[0])
    for cut in cuts[1:]:
        loudness = loudness * one(*cut)
    return loudness


def centred(own_key, extent, width, bound, cuts=(), kind=jnp.bfloat16):
    array = jax.random.normal(own_key, extent, jnp.float32) * width
    if len(cuts) > 0:
        array = levels(own_key, extent, cuts, -0.22, 0.18) * array
    return jnp.clip(array, min=-bound, max=bound).astype(kind)


def setup_inputs(seed: int = 0) -> dict:
    arg_keys = jax.random.split(jax.random.key(seed), 11)
    fwd_state = centred(arg_keys[0], (N_PIPE, TOKENS, D), 1.0, 6.0, ((0, 16), (1, 32)))
    rev_state = centred(arg_keys[1], (N_PIPE, TOKENS, D), 1.0, 6.0, ((0, 16), (1, 32)))
    norm_gain = jnp.clip(1.0 + 0.1 * jax.random.normal(arg_keys[2], (N_PIPE, D), jnp.float32), 0.5, 1.5)
    w_gate = centred(arg_keys[3], (N_PIPE, D, E_FLY * MOE_FF), D ** -0.5, 0.09375, ((0, 16), (2, 32)))
    w_up = centred(arg_keys[4], (N_PIPE, D, E_FLY * MOE_FF), D ** -0.5, 0.09375, ((0, 16), (2, 32)))
    w_down = centred(arg_keys[5], (N_PIPE, E_FLY * MOE_FF, D), MOE_FF ** -0.5, 0.1875, ((0, 16), (1, 32)))
    routes_fwd = draw_routes_fwd(jax.random.fold_in(arg_keys[10], 71), 0)
    scores_fwd = jnp.clip(jnp.exp(math.log(1.0) - 3.912023 * jax.random.uniform(arg_keys[7], (STEPS, N_PIPE, TOKENS, TOPK), jnp.float32) ** levels(arg_keys[7], (STEPS, N_PIPE, TOKENS, TOPK), ((1, 16), (2, 32)), -0.2, 0.2)), 0.02, 1.0)
    routes_rev = draw_routes_rev(jax.random.fold_in(arg_keys[10], 71), 0)
    scores_rev = jnp.clip(jnp.exp(math.log(1.0) - 3.912023 * jax.random.uniform(arg_keys[9], (STEPS, N_PIPE, TOKENS, TOPK), jnp.float32) ** levels(arg_keys[9], (STEPS, N_PIPE, TOKENS, TOPK), ((1, 16), (2, 32)), -0.2, 0.2)), 0.02, 1.0)
    return {"fwd_state": fwd_state, "rev_state": rev_state, "norm_gain": norm_gain, "w_gate": w_gate, "w_up": w_up, "w_down": w_down, "routes_fwd": routes_fwd, "scores_fwd": scores_fwd, "routes_rev": routes_rev, "scores_rev": scores_rev}


EPSILON = 1e-06
ROUTE_SCALE = 2.5

def normalize(tok_rows, gain_row):
    values = tok_rows.astype(jnp.float32)
    factor = lax.rsqrt(lax.optimization_barrier(jnp.mean(values * values, axis=-1, keepdims=True)) + EPSILON)
    return (values * factor * gain_row).astype(jnp.bfloat16)

def slot_tables(route_ids, route_scores, flying):
    expert_ids = jnp.arange(flying, dtype=jnp.int32)
    matches = (route_ids[:, :, None] == expert_ids[None, None, :]).astype(jnp.float32)
    hit_mask = lax.optimization_barrier(jnp.sum(matches, axis=1))
    weighted = ROUTE_SCALE * lax.optimization_barrier(jnp.sum(matches * route_scores[:, :, None], axis=1)) / lax.optimization_barrier(jnp.sum(route_scores, axis=1, keepdims=True))
    slot_index = jnp.cumsum(hit_mask, axis=0) - 1.0
    slot_ids = jnp.arange(CAP, dtype=jnp.float32)
    placed = hit_mask.T[:, None, :] * (slot_index.T[:, None, :] == slot_ids[None, :, None]).astype(jnp.float32)
    mix_table = placed * weighted.T[:, None, :]
    return (placed, mix_table)

def dispatch_slots(normed, placed):
    return jnp.einsum('ecr,rd->ecd', placed, normed.astype(jnp.float32), precision=lax.Precision.HIGHEST).astype(jnp.bfloat16)

def finish(tok_rows, summed, mix_table):
    added = jnp.einsum('ecr,ecd->rd', mix_table, summed, precision=lax.Precision.HIGHEST)
    return (tok_rows.astype(jnp.float32) + added).astype(jnp.bfloat16)

def section_layer(current, gain_row, gate_cols, up_cols, down_rows, route_ids, route_scores):
    blocks = current.reshape(N_EXPERT, TOK_DEV, D)
    id_blocks = route_ids.reshape(N_EXPERT, TOK_DEV, TOPK)
    score_blocks = route_scores.reshape(N_EXPERT, TOK_DEV, TOPK)
    normed = jax.vmap(normalize, in_axes=(0, None))(blocks, gain_row)
    placed, mix_table = jax.vmap(functools.partial(slot_tables, flying=E_FLY))(id_blocks, score_blocks)
    slot_rows = jax.vmap(dispatch_slots)(normed, placed)
    summed_list = []
    for expert in range(E_FLY):
        chosen = slot_rows[:, expert].reshape(N_EXPERT * CAP, D)
        lowest = expert * MOE_FF
        gate_act = jnp.dot(chosen, gate_cols[:, lowest:lowest + MOE_FF], preferred_element_type=jnp.float32)
        up_act = jnp.dot(chosen, up_cols[:, lowest:lowest + MOE_FF], preferred_element_type=jnp.float32)
        hidden = (jax.nn.silu(gate_act) * up_act).astype(jnp.bfloat16)
        down_part = down_rows[lowest:lowest + MOE_FF].reshape(SPLIT, HID_DEV, D).astype(jnp.float32)
        pieces = jnp.einsum('rsh,shd->rsd', hidden.reshape(N_EXPERT * CAP, SPLIT, HID_DEV).astype(jnp.float32), down_part)
        rounded = lax.optimization_barrier(pieces.astype(jnp.bfloat16))
        summed = lax.optimization_barrier(jnp.sum(rounded.astype(jnp.float32), axis=1))
        summed_list.append(summed.reshape(N_EXPERT, CAP, D))
    summed_all = jnp.stack(summed_list, axis=1)
    out_blocks = jax.vmap(finish)(blocks, summed_all, mix_table)
    return out_blocks.reshape(TOKENS, D)

def reference(fwd_state, rev_state, norm_gain, w_gate, w_up, w_down, routes_fwd, scores_fwd, routes_rev, scores_rev):

    def run_sections(states, route_ids, route_scores):

        def apply_section(packed):
            return section_layer(*packed)
        return lax.map(apply_section, (states, norm_gain, w_gate, w_up, w_down, route_ids, route_scores))
    forward_now = fwd_state
    reverse_now = rev_state
    for step_index in range(STEPS):
        forward_now = jnp.roll(run_sections(forward_now, routes_fwd[step_index], scores_fwd[step_index]), 1, axis=0)
        reverse_now = jnp.roll(run_sections(reverse_now, routes_rev[step_index], scores_rev[step_index]), -1, axis=0)
    return (forward_now, reverse_now)
```

```python
import jax
import jax.numpy as jnp
from jax import lax
from jax.sharding import Mesh, PartitionSpec as P

CAP = 4
STEPS = 3
GROUP = 4
PAIRS = 2

EPSILON = 1e-06
ROUTE_SCALE = 2.5


def shifted(value, axis, steps):
    count = lax.axis_size(axis)
    pairs = [(source, (source + steps) % count) for source in range(count)]
    return lax.ppermute(value, axis, pairs)


def normalize(tok_rows, gain_row):
    values = tok_rows.astype(jnp.float32)
    factor = lax.rsqrt(jnp.mean(values * values, axis=-1, keepdims=True) + EPSILON)
    return (values * factor * gain_row).astype(jnp.bfloat16)


def slot_tables(route_ids, route_scores, flying):
    expert_ids = jnp.arange(flying, dtype=jnp.int32)
    matches = (route_ids[:, :, None] == expert_ids[None, None, :]).astype(jnp.float32)
    hit_mask = jnp.sum(matches, axis=1)
    weighted = (
        ROUTE_SCALE
        * jnp.sum(matches * route_scores[:, :, None], axis=1)
        / jnp.sum(route_scores, axis=1, keepdims=True)
    )
    slot_index = jnp.cumsum(hit_mask, axis=0) - 1.0
    slot_ids = jnp.arange(CAP, dtype=jnp.float32)
    placed = hit_mask.T[:, None, :] * (slot_index.T[:, None, :] == slot_ids[None, :, None]).astype(
        jnp.float32
    )
    mix_table = placed * weighted.T[:, None, :]
    return (placed, mix_table)


def local(
    fwd_state,
    rev_state,
    norm_gain,
    w_gate,
    w_up,
    w_down,
    routes_fwd,
    scores_fwd,
    routes_rev,
    scores_rev,
):
    flying = lax.axis_size("g")
    pairs = lax.axis_size("h")
    width = fwd_state.shape[2]
    gain_row = norm_gain[0]

    def widened(block, axis):
        near = shifted(block, "b", 1)
        return jnp.concatenate(
            [block, shifted(block, "c", 1), near, shifted(near, "c", 1)], axis=axis
        )

    gate_cols = widened(w_gate[0], 1)
    up_cols = widened(w_up[0], 1)
    down_rows = widened(w_down[0], 0)

    def exchange(blocks):
        return lax.all_to_all(blocks, ("g", "h"), split_axis=0, concat_axis=0, tiled=True)

    def expert_partial(received):
        tok_rows = received.reshape(-1, width)
        gate_act = jnp.dot(tok_rows, gate_cols, preferred_element_type=jnp.float32)
        up_act = jnp.dot(tok_rows, up_cols, preferred_element_type=jnp.float32)
        hidden = (jax.nn.silu(gate_act) * up_act).astype(jnp.bfloat16)
        partial_out = jnp.dot(hidden, down_rows, preferred_element_type=jnp.float32).astype(
            jnp.bfloat16
        )
        return partial_out.reshape(received.shape)

    def prepare(current, tables):
        normed = normalize(current, gain_row)
        placed = tables[0].astype(jnp.bfloat16)
        slot_rows = jnp.einsum(
            "ecr,rd->ecd", placed, normed, preferred_element_type=jnp.float32
        ).astype(jnp.bfloat16)
        return jnp.broadcast_to(slot_rows[:, None], (flying, pairs, CAP, width)).reshape(
            flying * pairs, CAP, width
        )

    def finish(current, returned, tables):
        summed = jnp.sum(
            returned.astype(jnp.float32).reshape(flying, pairs, CAP, width), axis=1
        )
        added = jnp.einsum("ecr,ecd->rd", tables[1], summed, precision=lax.Precision.HIGHEST)
        return (current.astype(jnp.float32) + added).astype(jnp.bfloat16)

    fwd_tables = [slot_tables(routes_fwd[t, 0], scores_fwd[t, 0], flying) for t in range(STEPS)]
    rev_tables = [slot_tables(routes_rev[t, 0], scores_rev[t, 0], flying) for t in range(STEPS)]
    forward_now = fwd_state[0]
    reverse_now = rev_state[0]
    for t in range(STEPS):
        fwd_got = exchange(prepare(forward_now, fwd_tables[t]))
        rev_got = exchange(prepare(reverse_now, rev_tables[t]))
        fwd_back = exchange(expert_partial(fwd_got))
        forward_now = shifted(finish(forward_now, fwd_back, fwd_tables[t]), "pipe", 1)
        rev_back = exchange(expert_partial(rev_got))
        reverse_now = shifted(finish(reverse_now, rev_back, rev_tables[t]), "pipe", -1)
    return (forward_now[None], reverse_now[None])


def solution(mesh):
    pipe, expert = mesh.devices.shape
    devices = mesh.devices.reshape(pipe, GROUP, expert // (GROUP * PAIRS * 2), PAIRS, 2)
    split = Mesh(devices, ("pipe", "g", "h", "b", "c"))
    column = ("g", "h", "b", "c")
    in_specs = (
        P("pipe", column, None),
        P("pipe", column, None),
        P("pipe", None),
        P("pipe", None, column),
        P("pipe", None, column),
        P("pipe", column, None),
        P(None, "pipe", column, None),
        P(None, "pipe", column, None),
        P(None, "pipe", column, None),
        P(None, "pipe", column, None),
    )
    out_specs = (P("pipe", column, None), P("pipe", column, None))
    return jax.shard_map(local, mesh=split, in_specs=in_specs, out_specs=out_specs, check_vma=False)
```

```python
import jax
import jax.numpy as jnp
from jax import lax
from jax.sharding import Mesh, PartitionSpec as P

CAP = 4
STEPS = 3
GROUP = 4
PAIRS = 2

EPSILON = 1e-06
ROUTE_SCALE = 2.5


def shifted(value, axis, steps):
    count = lax.axis_size(axis)
    pairs = [(source, (source + steps) % count) for source in range(count)]
    return lax.ppermute(value, axis, pairs)


def normalize(tok_rows, gain_row):
    values = tok_rows.astype(jnp.float32)
    factor = lax.rsqrt(jnp.mean(values * values, axis=-1, keepdims=True) + EPSILON)
    return (values * factor * gain_row).astype(jnp.bfloat16)


def slot_tables(route_ids, route_scores, flying):
    expert_ids = jnp.arange(flying, dtype=jnp.int32)
    matches = (route_ids[:, :, None] == expert_ids[None, None, :]).astype(jnp.float32)
    hit_mask = jnp.sum(matches, axis=1)
    weighted = (
        ROUTE_SCALE
        * jnp.sum(matches * route_scores[:, :, None], axis=1)
        / jnp.sum(route_scores, axis=1, keepdims=True)
    )
    slot_index = jnp.cumsum(hit_mask, axis=0) - 1.0
    slot_ids = jnp.arange(CAP, dtype=jnp.float32)
    placed = hit_mask.T[:, None, :] * (slot_index.T[:, None, :] == slot_ids[None, :, None]).astype(
        jnp.float32
    )
    mix_table = placed * weighted.T[:, None, :]
    return (placed, mix_table)


def local(
    fwd_state,
    rev_state,
    norm_gain,
    w_gate,
    w_up,
    w_down,
    routes_fwd,
    scores_fwd,
    routes_rev,
    scores_rev,
):
    flying = lax.axis_size("g")
    pairs = lax.axis_size("h")
    width = fwd_state.shape[2]
    gain_row = norm_gain[0]

    def widened(block, axis):
        return jnp.concatenate([block, shifted(block, "c", 1)], axis=axis)

    gate_cols = widened(w_gate[0], 1)
    up_cols = widened(w_up[0], 1)
    down_rows = widened(w_down[0], 0)

    def exchange(blocks):
        return lax.all_to_all(blocks, ("g", "h"), split_axis=0, concat_axis=0, tiled=True)

    def partial_of(received):
        tok_rows = received.reshape(-1, width)
        gate_act = jnp.dot(tok_rows, gate_cols, preferred_element_type=jnp.float32)
        up_act = jnp.dot(tok_rows, up_cols, preferred_element_type=jnp.float32)
        hidden = (jax.nn.silu(gate_act) * up_act).astype(jnp.bfloat16)
        return jnp.dot(hidden, down_rows, preferred_element_type=jnp.float32)

    def expert_partial(received):
        near_rows = shifted(received, "b", 1)
        own_part = partial_of(received)
        near_part = partial_of(near_rows).astype(jnp.bfloat16)
        back_part = shifted(near_part, "b", 1)
        both = (own_part + back_part.astype(jnp.float32)).astype(jnp.bfloat16)
        return both.reshape(received.shape)

    def prepare(current, tables):
        normed = normalize(current, gain_row)
        placed = tables[0].astype(jnp.bfloat16)
        slot_rows = jnp.einsum(
            "ecr,rd->ecd", placed, normed, preferred_element_type=jnp.float32
        ).astype(jnp.bfloat16)
        return jnp.broadcast_to(slot_rows[:, None], (flying, pairs, CAP, width)).reshape(
            flying * pairs, CAP, width
        )

    def finish(current, returned, tables):
        summed = jnp.sum(
            returned.astype(jnp.float32).reshape(flying, pairs, CAP, width), axis=1
        )
        added = jnp.einsum("ecr,ecd->rd", tables[1], summed, precision=lax.Precision.HIGHEST)
        return (current.astype(jnp.float32) + added).astype(jnp.bfloat16)

    fwd_tables = [slot_tables(routes_fwd[t, 0], scores_fwd[t, 0], flying) for t in range(STEPS)]
    rev_tables = [slot_tables(routes_rev[t, 0], scores_rev[t, 0], flying) for t in range(STEPS)]
    forward_now = fwd_state[0]
    reverse_now = rev_state[0]
    for t in range(STEPS):
        fwd_got = exchange(prepare(forward_now, fwd_tables[t]))
        rev_got = exchange(prepare(reverse_now, rev_tables[t]))
        fwd_back = exchange(expert_partial(fwd_got))
        forward_now = shifted(finish(forward_now, fwd_back, fwd_tables[t]), "pipe", 1)
        rev_back = exchange(expert_partial(rev_got))
        reverse_now = shifted(finish(reverse_now, rev_back, rev_tables[t]), "pipe", -1)
    return (forward_now[None], reverse_now[None])


def solution(mesh):
    pipe, expert = mesh.devices.shape
    devices = mesh.devices.reshape(pipe, GROUP, expert // (GROUP * PAIRS * 2), PAIRS, 2)
    split = Mesh(devices, ("pipe", "g", "h", "b", "c"))
    column = ("g", "h", "b", "c")
    in_specs = (
        P("pipe", column, None),
        P("pipe", column, None),
        P("pipe", None),
        P("pipe", None, column),
        P("pipe", None, column),
        P("pipe", column, None),
        P(None, "pipe", column, None),
        P(None, "pipe", column, None),
        P(None, "pipe", column, None),
        P(None, "pipe", column, None),
    )
    out_specs = (P("pipe", column, None), P("pipe", column, None))
    return jax.shard_map(local, mesh=split, in_specs=in_specs, out_specs=out_specs, check_vma=False)
```

```python
import jax
import jax.numpy as jnp
from jax import lax
from jax.sharding import Mesh, PartitionSpec as P

CAP = 4
STEPS = 3
GROUP = 4
PAIRS = 2

EPSILON = 1e-06
ROUTE_SCALE = 2.5


def shifted(value, axis, steps):
    count = lax.axis_size(axis)
    pairs = [(source, (source + steps) % count) for source in range(count)]
    return lax.ppermute(value, axis, pairs)


def normalize(tok_rows, gain_row):
    values = tok_rows.astype(jnp.float32)
    factor = lax.rsqrt(jnp.mean(values * values, axis=-1, keepdims=True) + EPSILON)
    return (values * factor * gain_row).astype(jnp.bfloat16)


def slot_tables(route_ids, route_scores, flying):
    expert_ids = jnp.arange(flying, dtype=jnp.int32)
    matches = (route_ids[:, :, None] == expert_ids[None, None, :]).astype(jnp.float32)
    hit_mask = jnp.sum(matches, axis=1)
    weighted = (
        ROUTE_SCALE
        * jnp.sum(matches * route_scores[:, :, None], axis=1)
        / jnp.sum(route_scores, axis=1, keepdims=True)
    )
    slot_index = jnp.cumsum(hit_mask, axis=0) - 1.0
    slot_ids = jnp.arange(CAP, dtype=jnp.float32)
    placed = hit_mask.T[:, None, :] * (slot_index.T[:, None, :] == slot_ids[None, :, None]).astype(
        jnp.float32
    )
    mix_table = placed * weighted.T[:, None, :]
    return (placed, mix_table)


def local(
    fwd_state,
    rev_state,
    norm_gain,
    w_gate,
    w_up,
    w_down,
    routes_fwd,
    scores_fwd,
    routes_rev,
    scores_rev,
):
    flying = lax.axis_size("g")
    pairs = lax.axis_size("h")
    width = fwd_state.shape[2]
    gain_row = norm_gain[0]

    def widened(block, axis):
        return jnp.concatenate([block, shifted(block, "c", 1)], axis=axis)

    gate_cols = widened(w_gate[0], 1)
    up_cols = widened(w_up[0], 1)
    down_rows = widened(w_down[0], 0)

    def exchange(blocks):
        return lax.all_to_all(blocks, ("g", "h"), split_axis=0, concat_axis=0, tiled=True)

    def partial_of(received):
        tok_rows = received.reshape(-1, width)
        gate_act = jnp.dot(tok_rows, gate_cols, preferred_element_type=jnp.float32)
        up_act = jnp.dot(tok_rows, up_cols, preferred_element_type=jnp.float32)
        hidden = (jax.nn.silu(gate_act) * up_act).astype(jnp.bfloat16)
        return jnp.dot(hidden, down_rows, preferred_element_type=jnp.float32)

    def after(value, *earlier):
        return lax.optimization_barrier((value, *earlier))[0]

    def neighbour_partial(received):
        near_rows = shifted(received, "b", 1)
        own_part = partial_of(received)
        near_part = partial_of(after(near_rows, own_part)).astype(jnp.bfloat16)
        return own_part, near_part

    def joined(own_part, near_part):
        back_part = shifted(near_part, "b", 1)
        both = (own_part + back_part.astype(jnp.float32)).astype(jnp.bfloat16)
        return both.reshape(flying * pairs, CAP, width)

    def prepare(current, tables):
        normed = normalize(current, gain_row)
        placed = tables[0].astype(jnp.bfloat16)
        slot_rows = jnp.einsum(
            "ecr,rd->ecd", placed, normed, preferred_element_type=jnp.float32
        ).astype(jnp.bfloat16)
        return jnp.broadcast_to(slot_rows[:, None], (flying, pairs, CAP, width)).reshape(
            flying * pairs, CAP, width
        )

    def finish(current, returned, tables):
        summed = jnp.sum(
            returned.astype(jnp.float32).reshape(flying, pairs, CAP, width), axis=1
        )
        added = jnp.einsum("ecr,ecd->rd", tables[1], summed, precision=lax.Precision.HIGHEST)
        return (current.astype(jnp.float32) + added).astype(jnp.bfloat16)

    fwd_tables = [slot_tables(routes_fwd[t, 0], scores_fwd[t, 0], flying) for t in range(STEPS)]
    rev_tables = [slot_tables(routes_rev[t, 0], scores_rev[t, 0], flying) for t in range(STEPS)]
    forward_now = fwd_state[0]
    reverse_now = rev_state[0]
    fwd_sent = prepare(forward_now, fwd_tables[0])
    rev_sent = prepare(reverse_now, rev_tables[0])
    for t in range(STEPS):
        last = t == STEPS - 1
        fwd_got = after(exchange(fwd_sent), rev_sent)
        rev_got = exchange(rev_sent)
        fwd_own, fwd_near = neighbour_partial(fwd_got)
        rev_own, rev_near = neighbour_partial(after(rev_got, fwd_near))
        fwd_back = exchange(joined(fwd_own, fwd_near))
        rev_back = exchange(joined(rev_own, rev_near))
        fwd_done = finish(forward_now, after(fwd_back, rev_near), fwd_tables[t])
        forward_now = shifted(fwd_done, "pipe", 1)
        if not last:
            fwd_sent = prepare(forward_now, fwd_tables[t + 1])
        rev_back = after(rev_back, fwd_done if last else fwd_sent)
        reverse_now = shifted(finish(reverse_now, rev_back, rev_tables[t]), "pipe", -1)
        if not last:
            rev_sent = prepare(reverse_now, rev_tables[t + 1])
    return (forward_now[None], reverse_now[None])


def solution(mesh):
    pipe, expert = mesh.devices.shape
    devices = mesh.devices.reshape(pipe, GROUP, expert // (GROUP * PAIRS * 2), PAIRS, 2)
    split = Mesh(devices, ("pipe", "g", "h", "b", "c"))
    column = ("g", "h", "b", "c")
    in_specs = (
        P("pipe", column, None),
        P("pipe", column, None),
        P("pipe", None),
        P("pipe", None, column),
        P("pipe", None, column),
        P("pipe", column, None),
        P(None, "pipe", column, None),
        P(None, "pipe", column, None),
        P(None, "pipe", column, None),
        P(None, "pipe", column, None),
    )
    out_specs = (P("pipe", column, None), P("pipe", column, None))
    return jax.shard_map(local, mesh=split, in_specs=in_specs, out_specs=out_specs, check_vma=False)
```

```python
import jax
import jax.numpy as jnp
from jax import lax
from jax.sharding import Mesh, PartitionSpec as P

CAP = 4
STEPS = 3
GROUP = 4
PAIRS = 2

EPSILON = 1e-06
ROUTE_SCALE = 2.5


def shifted(value, axis, steps):
    count = lax.axis_size(axis)
    pairs = [(source, (source + steps) % count) for source in range(count)]
    return lax.ppermute(value, axis, pairs)


def after(value, *earlier):
    return lax.optimization_barrier((value, *earlier))[0]


def exact_pick(table, rows):
    return jnp.dot(table.astype(jnp.bfloat16), rows, preferred_element_type=jnp.float32)


def route_tables(route_ids, route_scores, flying):
    expert_ids = jnp.arange(flying, dtype=jnp.int32)
    matches = (route_ids[..., None] == expert_ids).astype(jnp.float32)
    hits = jnp.sum(matches, axis=3)
    weighted = (
        ROUTE_SCALE
        * jnp.sum(matches * route_scores[..., None], axis=3)
        / jnp.sum(route_scores, axis=3)[..., None]
    )
    places = jnp.cumsum(hits, axis=2) - 1.0
    slot_ids = jnp.arange(CAP, dtype=jnp.float32)
    placed = hits[..., None] * (places[..., None] == slot_ids).astype(jnp.float32)
    mixed = placed * weighted[..., None]
    earlier = jnp.cumsum(hits, axis=3) - hits
    firsts = placed * (earlier == 0.0).astype(jnp.float32)[..., None]
    flat = hits.shape[:3] + (flying * CAP,)
    return placed.reshape(flat), mixed.reshape(flat), firsts.reshape(flat)


def local(
    fwd_state,
    rev_state,
    norm_gain,
    w_gate,
    w_up,
    w_down,
    routes_fwd,
    scores_fwd,
    routes_rev,
    scores_rev,
):
    flying = lax.axis_size("g")
    pairs = lax.axis_size("h")
    width = fwd_state.shape[2]
    slots = flying * CAP
    gain_row = norm_gain[0]
    ways = (1, -1)

    def widened(block, axis):
        near = shifted(block, "b", 1)
        return jnp.concatenate(
            [block, shifted(block, "c", 1), near, shifted(near, "c", 1)], axis=axis
        )

    def exchange(blocks):
        return lax.all_to_all(blocks, ("g", "h"), split_axis=0, concat_axis=0, tiled=True)

    def spread(per_expert, stream):
        by_expert = per_expert.reshape(flying, CAP, -1)
        empty = jnp.zeros_like(by_expert)
        both = (by_expert, empty) if stream == 0 else (empty, by_expert)
        return jnp.concatenate(both, axis=1).reshape(2 * slots, -1)

    placed, mixed, firsts = route_tables(
        jnp.stack([routes_fwd[:, 0], routes_rev[:, 0]]),
        jnp.stack([scores_fwd[:, 0], scores_rev[:, 0]]),
        flying,
    )
    placed = placed.swapaxes(2, 3)
    mixing = jnp.einsum("stkr,strq->stkq", placed, mixed, precision=lax.Precision.HIGHEST)
    mixing = [
        [spread(mixing[s, t].T, s).T for t in range(STEPS)] for s in range(2)
    ]
    heard = [shifted(firsts[s].astype(jnp.bfloat16), "pipe", ways[s]) for s in range(2)]
    heard = [value.astype(jnp.float32) for value in heard]
    kept = [1.0 - jnp.sum(value, axis=2) for value in heard]

    def wanted_from(s, t):
        if t == 0:
            return placed[s, 0], None
        return placed[s, t] * kept[s][t - 1], placed[s, t] @ heard[s][t - 1]

    def gathered(rows, changed, from_rows, from_changed):
        found = exact_pick(from_rows, rows)
        if changed is not None:
            found = found + exact_pick(from_changed, changed)
        return found

    def merged_rows(rows, changed, s, t):
        return (
            kept[s][t][:, None] * rows.astype(jnp.float32) + exact_pick(heard[s][t], changed)
        ).astype(jnp.bfloat16)

    gate_cols = widened(w_gate[0], 1)
    up_cols = widened(w_up[0], 1)
    down_rows = widened(w_down[0], 0)

    rows = [fwd_state[0], rev_state[0]]
    base = rows
    changed = [None, None]
    for t in range(STEPS):
        tables = [wanted_from(s, t) for s in range(2)]
        found = sum(
            gathered(
                base[s],
                changed[s],
                spread(tables[s][0], s),
                None if changed[s] is None else spread(tables[s][1], s),
            )
            for s in range(2)
        )
        factor = lax.rsqrt(jnp.mean(found * found, axis=-1, keepdims=True) + EPSILON)
        normed = (found * factor * gain_row).astype(jnp.bfloat16)
        sent = jnp.broadcast_to(
            normed.reshape(flying, 1, 2 * CAP, width), (flying, pairs, 2 * CAP, width)
        ).reshape(flying * pairs, 2 * CAP, width)
        got = exchange(sent)

        if t > 0:
            rows = [merged_rows(base[s], after(changed[s], sent), s, t - 1) for s in range(2)]
        next_base = [shifted(rows[s], "pipe", ways[s]) for s in range(2)]
        own = [exact_pick(placed[s, t], rows[s]) for s in range(2)]

        tok_rows = after(got, *own).reshape(-1, width)
        gate_act = jnp.dot(tok_rows, gate_cols, preferred_element_type=jnp.float32)
        up_act = jnp.dot(tok_rows, up_cols, preferred_element_type=jnp.float32)
        hidden = (jax.nn.silu(gate_act) * up_act).astype(jnp.bfloat16)
        part = jnp.dot(hidden, down_rows, preferred_element_type=jnp.float32).astype(jnp.bfloat16)
        back = exchange(part.reshape(flying * pairs, 2 * CAP, width))

        summed = jnp.sum(
            back.astype(jnp.float32).reshape(flying, pairs, 2 * CAP, width), axis=1
        ).reshape(2 * slots, width)
        changed = [
            shifted(
                (
                    own[s] + jnp.dot(mixing[s][t], summed, precision=lax.Precision.HIGHEST)
                ).astype(jnp.bfloat16),
                "pipe",
                ways[s],
            )
            for s in range(2)
        ]
        base = next_base
    out = [merged_rows(base[s], changed[s], s, STEPS - 1) for s in range(2)]
    return (out[0][None], out[1][None])


def solution(mesh):
    pipe, expert = mesh.devices.shape
    devices = mesh.devices.reshape(pipe, GROUP, expert // (GROUP * PAIRS * 2), PAIRS, 2)
    split = Mesh(devices, ("pipe", "g", "h", "b", "c"))
    column = ("g", "h", "b", "c")
    in_specs = (
        P("pipe", column, None),
        P("pipe", column, None),
        P("pipe", None),
        P("pipe", None, column),
        P("pipe", None, column),
        P("pipe", column, None),
        P(None, "pipe", column, None),
        P(None, "pipe", column, None),
        P(None, "pipe", column, None),
        P(None, "pipe", column, None),
    )
    out_specs = (P("pipe", column, None), P("pipe", column, None))
    return jax.shard_map(local, mesh=split, in_specs=in_specs, out_specs=out_specs, check_vma=False)
```

```python
import jax
import jax.numpy as jnp
from jax import lax
from jax.sharding import PartitionSpec as P

SPLIT = 8
CAP = 4
STEPS = 3

EPSILON = 1e-06
ROUTE_SCALE = 2.5


def shifted(value, axis, steps):
    count = lax.axis_size(axis)
    pairs = [(source, (source + steps) % count) for source in range(count)]
    return lax.ppermute(value, axis, pairs)


def swapped(value, bit):
    count = lax.axis_size("expert")
    return lax.ppermute(value, "expert", [(source, source ^ bit) for source in range(count)])


def pair_groups(count):
    pairs = count // 4
    return [
        [4 * pair + 2 * (side ^ (2 * pair // pairs)) + core for pair in range(pairs)]
        for side in range(2)
        for core in range(2)
    ]


def after(value, *earlier):
    return lax.optimization_barrier((value, *earlier))[0]


def exact_pick(table, rows):
    return jnp.dot(table.astype(jnp.bfloat16), rows, preferred_element_type=jnp.float32)


def route_tables(route_ids, route_scores, flying):
    expert_ids = jnp.arange(flying, dtype=jnp.int32)
    matches = (route_ids[..., None] == expert_ids).astype(jnp.float32)
    hits = jnp.sum(matches, axis=3)
    weighted = (
        ROUTE_SCALE
        * jnp.sum(matches * route_scores[..., None], axis=3)
        / jnp.sum(route_scores, axis=3)[..., None]
    )
    places = jnp.cumsum(hits, axis=2) - 1.0
    slot_ids = jnp.arange(CAP, dtype=jnp.float32)
    placed = hits[..., None] * (places[..., None] == slot_ids).astype(jnp.float32)
    mixed = placed * weighted[..., None]
    earlier = jnp.cumsum(hits, axis=3) - hits
    firsts = placed * (earlier == 0.0).astype(jnp.float32)[..., None]
    flat = hits.shape[:3] + (flying * CAP,)
    return placed.reshape(flat), mixed.reshape(flat), firsts.reshape(flat)


def local(
    fwd_state,
    rev_state,
    norm_gain,
    w_gate,
    w_up,
    w_down,
    routes_fwd,
    scores_fwd,
    routes_rev,
    scores_rev,
):
    count = lax.axis_size("expert")
    flying = count // SPLIT
    pairs = SPLIT // 4
    groups = pair_groups(count)
    width = fwd_state.shape[2]
    slots = flying * CAP
    gain_row = norm_gain[0]
    ways = (1, -1)

    def widened(block, axis):
        near = swapped(block, 2)
        return jnp.concatenate([block, swapped(block, 1), near, swapped(near, 1)], axis=axis)

    def exchange(blocks):
        return lax.all_to_all(
            blocks, "expert", split_axis=0, concat_axis=0, axis_index_groups=groups, tiled=True
        )

    def spread(per_expert, stream):
        by_expert = per_expert.reshape(flying, CAP, -1)
        empty = jnp.zeros_like(by_expert)
        both = (by_expert, empty) if stream == 0 else (empty, by_expert)
        return jnp.concatenate(both, axis=1).reshape(2 * slots, -1)

    placed, mixed, firsts = route_tables(
        jnp.stack([routes_fwd[:, 0], routes_rev[:, 0]]),
        jnp.stack([scores_fwd[:, 0], scores_rev[:, 0]]),
        flying,
    )
    placed = placed.swapaxes(2, 3)
    mixing = jnp.einsum("stkr,strq->stkq", placed, mixed, precision=lax.Precision.HIGHEST)
    mixing = [
        [spread(mixing[s, t].T, s).T for t in range(STEPS)] for s in range(2)
    ]
    heard = [shifted(firsts[s].astype(jnp.bfloat16), "pipe", ways[s]) for s in range(2)]
    heard = [value.astype(jnp.float32) for value in heard]
    kept = [1.0 - jnp.sum(value, axis=2) for value in heard]

    def wanted_from(s, t):
        if t == 0:
            return placed[s, 0], None
        return placed[s, t] * kept[s][t - 1], placed[s, t] @ heard[s][t - 1]

    def gathered(rows, changed, from_rows, from_changed):
        found = exact_pick(from_rows, rows)
        if changed is not None:
            found = found + exact_pick(from_changed, changed)
        return found

    def merged_rows(rows, changed, s, t):
        return (
            kept[s][t][:, None] * rows.astype(jnp.float32) + exact_pick(heard[s][t], changed)
        ).astype(jnp.bfloat16)

    gate_cols = widened(w_gate[0], 1)
    up_cols = widened(w_up[0], 1)
    down_rows = widened(w_down[0], 0)

    rows = [fwd_state[0], rev_state[0]]
    base = rows
    changed = [None, None]
    for t in range(STEPS):
        tables = [wanted_from(s, t) for s in range(2)]
        found = sum(
            gathered(
                base[s],
                changed[s],
                spread(tables[s][0], s),
                None if changed[s] is None else spread(tables[s][1], s),
            )
            for s in range(2)
        )
        factor = lax.rsqrt(jnp.mean(found * found, axis=-1, keepdims=True) + EPSILON)
        normed = (found * factor * gain_row).astype(jnp.bfloat16)
        sent = jnp.broadcast_to(
            normed.reshape(flying, 1, 2 * CAP, width), (flying, pairs, 2 * CAP, width)
        ).reshape(flying * pairs, 2 * CAP, width)
        got = exchange(sent)

        if t > 0:
            rows = [merged_rows(base[s], after(changed[s], sent), s, t - 1) for s in range(2)]
        next_base = [shifted(rows[s], "pipe", ways[s]) for s in range(2)]
        own = [exact_pick(placed[s, t], rows[s]) for s in range(2)]

        tok_rows = after(got, *own).reshape(-1, width)
        gate_act = jnp.dot(tok_rows, gate_cols, preferred_element_type=jnp.float32)
        up_act = jnp.dot(tok_rows, up_cols, preferred_element_type=jnp.float32)
        hidden = (jax.nn.silu(gate_act) * up_act).astype(jnp.bfloat16)
        part = jnp.dot(hidden, down_rows, preferred_element_type=jnp.float32).astype(jnp.bfloat16)
        back = exchange(part.reshape(flying * pairs, 2 * CAP, width))

        summed = jnp.sum(
            back.astype(jnp.float32).reshape(flying, pairs, 2 * CAP, width), axis=1
        ).reshape(2 * slots, width)
        changed = [
            shifted(
                (
                    own[s] + jnp.dot(mixing[s][t], summed, precision=lax.Precision.HIGHEST)
                ).astype(jnp.bfloat16),
                "pipe",
                ways[s],
            )
            for s in range(2)
        ]
        base = next_base
    out = [merged_rows(base[s], changed[s], s, STEPS - 1) for s in range(2)]
    return (out[0][None], out[1][None])


def solution(mesh):
    in_specs = (
        P("pipe", "expert", None),
        P("pipe", "expert", None),
        P("pipe", None),
        P("pipe", None, "expert"),
        P("pipe", None, "expert"),
        P("pipe", "expert", None),
        P(None, "pipe", "expert", None),
        P(None, "pipe", "expert", None),
        P(None, "pipe", "expert", None),
        P(None, "pipe", "expert", None),
    )
    out_specs = (P("pipe", "expert", None), P("pipe", "expert", None))
    return jax.shard_map(local, mesh=mesh, in_specs=in_specs, out_specs=out_specs, check_vma=False)
```

```python
import jax
import jax.numpy as jnp
from jax import lax
from jax.sharding import Mesh, PartitionSpec as P

CAP = 4
STEPS = 3
GROUP = 4
PAIRS = 2

EPSILON = 1e-06
ROUTE_SCALE = 2.5


def shifted(value, axis, steps):
    count = lax.axis_size(axis)
    pairs = [(source, (source + steps) % count) for source in range(count)]
    return lax.ppermute(value, axis, pairs)


def after(value, *earlier):
    return lax.optimization_barrier((value, *earlier))[0]


def exact_pick(table, rows):
    return jnp.dot(table.astype(jnp.bfloat16), rows, preferred_element_type=jnp.float32)


def route_tables(route_ids, route_scores, flying):
    expert_ids = jnp.arange(flying, dtype=jnp.int32)
    matches = (route_ids[..., None] == expert_ids).astype(jnp.float32)
    hits = jnp.sum(matches, axis=3)
    weighted = (
        ROUTE_SCALE
        * jnp.sum(matches * route_scores[..., None], axis=3)
        / jnp.sum(route_scores, axis=3)[..., None]
    )
    places = jnp.cumsum(hits, axis=2) - 1.0
    slot_ids = jnp.arange(CAP, dtype=jnp.float32)
    placed = hits[..., None] * (places[..., None] == slot_ids).astype(jnp.float32)
    mixed = placed * weighted[..., None]
    earlier = jnp.cumsum(hits, axis=3) - hits
    firsts = placed * (earlier == 0.0).astype(jnp.float32)[..., None]
    flat = hits.shape[:3] + (flying * CAP,)
    return placed.reshape(flat), mixed.reshape(flat), firsts.reshape(flat)


def relay(
    fwd_state,
    rev_state,
    norm_gain,
    w_gate,
    w_up,
    w_down,
    routes_fwd,
    scores_fwd,
    routes_rev,
    scores_rev,
):
    flying = lax.axis_size("g")
    pairs = lax.axis_size("h")
    width = fwd_state.shape[2]
    slots = flying * CAP
    gain_row = norm_gain[0]
    ways = (1, -1)

    def widened(block, axis):
        near = shifted(block, "b", 1)
        return jnp.concatenate(
            [block, shifted(block, "c", 1), near, shifted(near, "c", 1)], axis=axis
        )

    def exchange(blocks):
        return lax.all_to_all(blocks, ("g", "h"), split_axis=0, concat_axis=0, tiled=True)

    def spread(per_expert, stream, copies):
        by_expert = per_expert.reshape(flying, CAP, -1)
        empty = jnp.zeros_like(by_expert)
        both = (by_expert, empty) if stream == 0 else (empty, by_expert)
        both = jnp.concatenate(both, axis=1)[:, None]
        return jnp.broadcast_to(both, (flying, copies) + both.shape[2:]).reshape(
            flying * copies * 2 * CAP, -1
        )

    placed, mixed, firsts = route_tables(
        jnp.stack([routes_fwd[:, 0], routes_rev[:, 0]]),
        jnp.stack([scores_fwd[:, 0], scores_rev[:, 0]]),
        flying,
    )
    placed = placed.swapaxes(2, 3)
    mixing = jnp.einsum("stkr,strq->stkq", placed, mixed, precision=lax.Precision.HIGHEST)
    mixing = [
        [spread(mixing[s, t].T, s, 1).T for t in range(STEPS)] for s in range(2)
    ]
    heard = [shifted(firsts[s].astype(jnp.bfloat16), "pipe", ways[s]) for s in range(2)]
    heard = [value.astype(jnp.float32) for value in heard]
    kept = [1.0 - jnp.sum(value, axis=2) for value in heard]

    def wanted_from(s, t):
        if t == 0:
            return placed[s, 0], None
        return placed[s, t] * kept[s][t - 1], placed[s, t] @ heard[s][t - 1]

    def gathered(rows, changed, from_rows, from_changed):
        found = exact_pick(from_rows, rows)
        if changed is not None:
            found = found + exact_pick(from_changed, changed)
        return found

    def merged_rows(rows, changed, s, t):
        return (
            kept[s][t][:, None] * rows.astype(jnp.float32) + exact_pick(heard[s][t], changed)
        ).astype(jnp.bfloat16)

    gate_cols = widened(w_gate[0], 1)
    up_cols = widened(w_up[0], 1)
    down_rows = widened(w_down[0], 0)
    rows = [fwd_state[0], rev_state[0]]
    base = rows
    changed = [None, None]
    for t in range(STEPS):
        tables = [wanted_from(s, t) for s in range(2)]
        found = sum(
            gathered(
                base[s],
                changed[s],
                spread(tables[s][0], s, pairs),
                None if changed[s] is None else spread(tables[s][1], s, pairs),
            )
            for s in range(2)
        )
        factor = lax.rsqrt(jnp.mean(found * found, axis=-1, keepdims=True) + EPSILON)
        normed = (found * factor * gain_row).astype(jnp.bfloat16)
        sent = normed.reshape(flying * pairs, 2 * CAP, width)
        got = exchange(sent)

        if t > 0:
            rows = [merged_rows(base[s], after(changed[s], sent), s, t - 1) for s in range(2)]
        next_base = [shifted(rows[s], "pipe", ways[s]) for s in range(2)]
        own = [exact_pick(placed[s, t], rows[s]) for s in range(2)]

        tok_rows = after(got, *own).reshape(-1, width)
        gate_act = jnp.dot(tok_rows, gate_cols, preferred_element_type=jnp.float32)
        up_act = jnp.dot(tok_rows, up_cols, preferred_element_type=jnp.float32)
        hidden = after((jax.nn.silu(gate_act) * up_act).astype(jnp.bfloat16))
        part = jnp.dot(hidden, down_rows, preferred_element_type=jnp.float32).astype(jnp.bfloat16)
        back = exchange(part.reshape(flying * pairs, 2 * CAP, width))

        summed = jnp.sum(
            back.astype(jnp.float32).reshape(flying, pairs, 2 * CAP, width), axis=1
        ).reshape(2 * slots, width)
        changed = [
            shifted(
                (
                    own[s] + jnp.dot(mixing[s][t], summed, precision=lax.Precision.HIGHEST)
                ).astype(jnp.bfloat16),
                "pipe",
                ways[s],
            )
            for s in range(2)
        ]
        base = next_base
    out = [merged_rows(base[s], changed[s], s, STEPS - 1) for s in range(2)]
    return (out[0][None], out[1][None])


def solution(mesh):
    pipe, expert = mesh.devices.shape
    devices = mesh.devices.reshape(pipe, GROUP, expert // (GROUP * PAIRS * 2), PAIRS, 2)
    split = Mesh(devices, ("pipe", "g", "h", "b", "c"))
    column = ("g", "h", "b", "c")
    in_specs = (
        P("pipe", column, None),
        P("pipe", column, None),
        P("pipe", None),
        P("pipe", None, column),
        P("pipe", None, column),
        P("pipe", column, None),
        P(None, "pipe", column, None),
        P(None, "pipe", column, None),
        P(None, "pipe", column, None),
        P(None, "pipe", column, None),
    )
    out_specs = (P("pipe", column, None), P("pipe", column, None))
    return jax.shard_map(relay, mesh=split, in_specs=in_specs, out_specs=out_specs, check_vma=False)
```

```python
import jax
import jax.numpy as jnp
from jax import lax
from jax.sharding import Mesh, PartitionSpec as P

CAP = 4
STEPS = 3
GROUP = 4
PAIRS = 2

EPSILON = 1e-06
ROUTE_SCALE = 2.5


def shifted(value, axis, steps):
    count = lax.axis_size(axis)
    pairs = [(source, (source + steps) % count) for source in range(count)]
    return lax.ppermute(value, axis, pairs)


def after(value, *earlier):
    return lax.optimization_barrier((value, *earlier))[0]


def exact_pick(table, rows):
    return jnp.dot(table.astype(jnp.bfloat16), rows, preferred_element_type=jnp.float32)


def route_tables(route_ids, route_scores, flying):
    expert_ids = jnp.arange(flying, dtype=jnp.int32)
    matches = (route_ids[..., None] == expert_ids).astype(jnp.float32)
    hits = jnp.sum(matches, axis=3)
    weighted = (
        ROUTE_SCALE
        * jnp.sum(matches * route_scores[..., None], axis=3)
        / jnp.sum(route_scores, axis=3)[..., None]
    )
    places = jnp.cumsum(hits, axis=2) - 1.0
    slot_ids = jnp.arange(CAP, dtype=jnp.float32)
    placed = hits[..., None] * (places[..., None] == slot_ids).astype(jnp.float32)
    mixed = placed * weighted[..., None]
    earlier = jnp.cumsum(hits, axis=3) - hits
    firsts = placed * (earlier == 0.0).astype(jnp.float32)[..., None]
    flat = hits.shape[:3] + (flying * CAP,)
    return placed.reshape(flat), mixed.reshape(flat), firsts.reshape(flat)


def relay(
    fwd_state,
    rev_state,
    norm_gain,
    w_gate,
    w_up,
    w_down,
    routes_fwd,
    scores_fwd,
    routes_rev,
    scores_rev,
):
    flying = lax.axis_size("g")
    pairs = lax.axis_size("h")
    width = fwd_state.shape[2]
    slots = flying * CAP
    gain_row = norm_gain[0]
    ways = (1, -1)

    def widened(block, axis):
        near = shifted(block, "b", 1)
        return jnp.concatenate(
            [block, shifted(block, "c", 1), near, shifted(near, "c", 1)], axis=axis
        )

    def exchange(blocks):
        return lax.all_to_all(blocks, ("g", "h"), split_axis=0, concat_axis=0, tiled=True)

    def spread(per_expert, stream):
        by_expert = per_expert.reshape(flying, CAP, -1)
        empty = jnp.zeros_like(by_expert)
        both = (by_expert, empty) if stream == 0 else (empty, by_expert)
        return jnp.concatenate(both, axis=1).reshape(2 * slots, -1)

    placed, mixed, firsts = route_tables(
        jnp.stack([routes_fwd[:, 0], routes_rev[:, 0]]),
        jnp.stack([scores_fwd[:, 0], scores_rev[:, 0]]),
        flying,
    )
    placed = placed.swapaxes(2, 3)
    mixing = jnp.einsum("stkr,strq->stkq", placed, mixed, precision=lax.Precision.HIGHEST)
    mixing = [
        [spread(mixing[s, t].T, s).T for t in range(STEPS)] for s in range(2)
    ]
    heard = [shifted(firsts[s].astype(jnp.bfloat16), "pipe", ways[s]) for s in range(2)]
    heard = [value.astype(jnp.float32) for value in heard]
    kept = [1.0 - jnp.sum(value, axis=2) for value in heard]

    def wanted_from(s, t):
        if t == 0:
            return placed[s, 0], None
        return placed[s, t] * kept[s][t - 1], placed[s, t] @ heard[s][t - 1]

    def gathered(rows, changed, from_rows, from_changed):
        found = exact_pick(from_rows, rows)
        if changed is not None:
            found = found + exact_pick(from_changed, changed)
        return found

    def merged_rows(rows, changed, s, t):
        return (
            kept[s][t][:, None] * rows.astype(jnp.float32) + exact_pick(heard[s][t], changed)
        ).astype(jnp.bfloat16)

    gate_cols = widened(w_gate[0], 1)
    up_cols = widened(w_up[0], 1)
    down_rows = widened(w_down[0], 0)

    rows = [fwd_state[0], rev_state[0]]
    base = rows
    changed = [None, None]
    for t in range(STEPS):
        tables = [wanted_from(s, t) for s in range(2)]
        found = sum(
            gathered(
                base[s],
                changed[s],
                spread(tables[s][0], s),
                None if changed[s] is None else spread(tables[s][1], s),
            )
            for s in range(2)
        )
        factor = lax.rsqrt(jnp.mean(found * found, axis=-1, keepdims=True) + EPSILON)
        normed = (found * factor * gain_row).astype(jnp.bfloat16)
        sent = jnp.broadcast_to(
            normed.reshape(flying, 1, 2 * CAP, width), (flying, pairs, 2 * CAP, width)
        ).reshape(flying * pairs, 2 * CAP, width)
        got = exchange(sent)

        if t > 0:
            rows = [merged_rows(base[s], after(changed[s], sent), s, t - 1) for s in range(2)]
        next_base = [shifted(rows[s], "pipe", ways[s]) for s in range(2)]
        own = [exact_pick(placed[s, t], rows[s]) for s in range(2)]

        tok_rows = after(got, *own).reshape(-1, width)
        gate_act = jnp.dot(tok_rows, gate_cols, preferred_element_type=jnp.float32)
        up_act = jnp.dot(tok_rows, up_cols, preferred_element_type=jnp.float32)
        hidden = (jax.nn.silu(gate_act) * up_act).astype(jnp.bfloat16)
        part = jnp.dot(hidden, down_rows, preferred_element_type=jnp.float32)
        part = part.astype(jnp.bfloat16)
        back = exchange(part.reshape(flying * pairs, 2 * CAP, width))

        summed = jnp.sum(
            back.astype(jnp.float32).reshape(flying, pairs, 2 * CAP, width), axis=1
        ).reshape(2 * slots, width)
        changed = [
            shifted(
                (
                    own[s] + jnp.dot(mixing[s][t], summed, precision=lax.Precision.HIGHEST)
                ).astype(jnp.bfloat16),
                "pipe",
                ways[s],
            )
            for s in range(2)
        ]
        base = next_base
    out = [merged_rows(base[s], changed[s], s, STEPS - 1) for s in range(2)]
    return (out[0][None], out[1][None])


def solution(mesh):
    pipe, expert = mesh.devices.shape
    devices = mesh.devices.reshape(pipe, GROUP, expert // (GROUP * PAIRS * 2), PAIRS, 2)
    split = Mesh(devices, ("pipe", "g", "h", "b", "c"))
    column = ("g", "h", "b", "c")
    in_specs = (
        P("pipe", column, None),
        P("pipe", column, None),
        P("pipe", None),
        P("pipe", None, column),
        P("pipe", None, column),
        P("pipe", column, None),
        P(None, "pipe", column, None),
        P(None, "pipe", column, None),
        P(None, "pipe", column, None),
        P(None, "pipe", column, None),
    )
    out_specs = (P("pipe", column, None), P("pipe", column, None))
    return jax.shard_map(relay, mesh=split, in_specs=in_specs, out_specs=out_specs, check_vma=False)
```

```python
import jax
import jax.numpy as jnp
from jax import lax
from jax.sharding import Mesh, PartitionSpec as P

CAP = 4
STEPS = 3
GROUP = 4
PAIRS = 2

EPSILON = 1e-06
ROUTE_SCALE = 2.5


def shifted(value, axis, steps):
    count = lax.axis_size(axis)
    pairs = [(source, (source + steps) % count) for source in range(count)]
    return lax.ppermute(value, axis, pairs)


def after(value, *earlier):
    return lax.optimization_barrier((value, *earlier))[0]


def exact_pick(table, rows):
    return jnp.dot(table.astype(jnp.bfloat16), rows, preferred_element_type=jnp.float32)


def route_tables(route_ids, route_scores, flying):
    expert_ids = jnp.arange(flying, dtype=jnp.int32)
    matches = (route_ids[..., None] == expert_ids).astype(jnp.float32)
    hits = jnp.sum(matches, axis=3)
    weighted = (
        ROUTE_SCALE
        * jnp.sum(matches * route_scores[..., None], axis=3)
        / jnp.sum(route_scores, axis=3)[..., None]
    )
    places = jnp.cumsum(hits, axis=2) - 1.0
    slot_ids = jnp.arange(CAP, dtype=jnp.float32)
    placed = hits[..., None] * (places[..., None] == slot_ids).astype(jnp.float32)
    mixed = placed * weighted[..., None]
    earlier = jnp.cumsum(hits, axis=3) - hits
    firsts = placed * (earlier == 0.0).astype(jnp.float32)[..., None]
    flat = hits.shape[:3] + (flying * CAP,)
    return placed.reshape(flat), mixed.reshape(flat), firsts.reshape(flat)


def relay(
    fwd_state,
    rev_state,
    norm_gain,
    w_gate,
    w_up,
    w_down,
    routes_fwd,
    scores_fwd,
    routes_rev,
    scores_rev,
):
    flying = lax.axis_size("g")
    pairs = lax.axis_size("h")
    width = fwd_state.shape[2]
    slots = flying * CAP
    gain_row = norm_gain[0]
    ways = (1, -1)

    def widened(block, axis):
        near = shifted(block, "b", 1)
        other = shifted(block, "c", 1)
        return jnp.concatenate([block, other, near, shifted(near, "c", 1)], axis=axis)

    def exchange(blocks):
        return lax.all_to_all(blocks, ("g", "h"), split_axis=0, concat_axis=0, tiled=True)

    def spread(per_expert, stream):
        by_expert = per_expert.reshape(flying, CAP, -1)
        empty = jnp.zeros_like(by_expert)
        both = (by_expert, empty) if stream == 0 else (empty, by_expert)
        return jnp.concatenate(both, axis=1).reshape(2 * slots, -1)

    placed, mixed, firsts = route_tables(
        jnp.stack([routes_fwd[:, 0], routes_rev[:, 0]]),
        jnp.stack([scores_fwd[:, 0], scores_rev[:, 0]]),
        flying,
    )
    placed = placed.swapaxes(2, 3)
    mixing = jnp.einsum("stkr,strq->stkq", placed, mixed, precision=lax.Precision.HIGHEST)
    mixing = [
        [spread(mixing[s, t].T, s).T for t in range(STEPS)] for s in range(2)
    ]
    heard = [shifted(firsts[s].astype(jnp.bfloat16), "pipe", ways[s]) for s in range(2)]
    heard = [value.astype(jnp.float32) for value in heard]
    kept = [1.0 - jnp.sum(value, axis=2) for value in heard]

    def wanted_from(s, t):
        if t == 0:
            return placed[s, 0], None
        return placed[s, t] * kept[s][t - 1], placed[s, t] @ heard[s][t - 1]

    def gathered(rows, changed, from_rows, from_changed):
        found = exact_pick(from_rows, rows)
        if changed is not None:
            found = found + exact_pick(from_changed, changed)
        return found

    def merged_rows(rows, changed, s, t):
        return (
            kept[s][t][:, None] * rows.astype(jnp.float32) + exact_pick(heard[s][t], changed)
        ).astype(jnp.bfloat16)

    gate_cols = widened(w_gate[0], 1)
    up_cols = widened(w_up[0], 1)
    down_rows = widened(w_down[0], 0)

    rows = [fwd_state[0], rev_state[0]]
    base = rows
    changed = [None, None]
    for t in range(STEPS):
        tables = [wanted_from(s, t) for s in range(2)]
        found = sum(
            gathered(
                base[s],
                changed[s],
                spread(tables[s][0], s),
                None if changed[s] is None else spread(tables[s][1], s),
            )
            for s in range(2)
        )
        factor = lax.rsqrt(jnp.mean(found * found, axis=-1, keepdims=True) + EPSILON)
        normed = (found * factor * gain_row).astype(jnp.bfloat16)
        sent = jnp.broadcast_to(
            normed.reshape(flying, 1, 2 * CAP, width), (flying, pairs, 2 * CAP, width)
        ).reshape(flying * pairs, 2 * CAP, width)
        got = exchange(sent)

        if t > 0:
            rows = [merged_rows(base[s], after(changed[s], sent), s, t - 1) for s in range(2)]
        next_base = [shifted(rows[s], "pipe", ways[s]) for s in range(2)]
        own = [exact_pick(placed[s, t], rows[s]) for s in range(2)]

        tok_rows = after(got, *own).reshape(-1, width)
        gate_act = jnp.dot(tok_rows, gate_cols, preferred_element_type=jnp.float32)
        up_act = jnp.dot(tok_rows, up_cols, preferred_element_type=jnp.float32)
        hidden = (jax.nn.silu(gate_act) * up_act).astype(jnp.bfloat16)
        part = jnp.dot(hidden, down_rows, preferred_element_type=jnp.float32).astype(jnp.bfloat16)
        back = exchange(part.reshape(flying * pairs, 2 * CAP, width))

        summed = jnp.sum(
            back.astype(jnp.float32).reshape(flying, pairs, 2 * CAP, width), axis=1
        ).reshape(2 * slots, width)
        changed = [
            shifted(
                (
                    own[s] + jnp.dot(mixing[s][t], summed, precision=lax.Precision.HIGHEST)
                ).astype(jnp.bfloat16),
                "pipe",
                ways[s],
            )
            for s in range(2)
        ]
        base = next_base
    out = [merged_rows(base[s], changed[s], s, STEPS - 1) for s in range(2)]
    return (out[0][None], out[1][None])


def solution(mesh):
    pipe, expert = mesh.devices.shape
    devices = mesh.devices.reshape(pipe, GROUP, expert // (GROUP * PAIRS * 2), PAIRS, 2)
    split = Mesh(devices, ("pipe", "g", "h", "b", "c"))
    column = ("g", "h", "b", "c")
    in_specs = (
        P("pipe", column, None),
        P("pipe", column, None),
        P("pipe", None),
        P("pipe", None, column),
        P("pipe", None, column),
        P("pipe", column, None),
        P(None, "pipe", column, None),
        P(None, "pipe", column, None),
        P(None, "pipe", column, None),
        P(None, "pipe", column, None),
    )
    out_specs = (P("pipe", column, None), P("pipe", column, None))
    return jax.shard_map(relay, mesh=split, in_specs=in_specs, out_specs=out_specs, check_vma=False)
```

```python
import jax
import jax.numpy as jnp
from jax import lax
from jax.sharding import Mesh, PartitionSpec as P

CAP = 4
STEPS = 3
GROUP = 4
PAIRS = 2

EPSILON = 1e-06
ROUTE_SCALE = 2.5


def shifted(value, axis, steps):
    count = lax.axis_size(axis)
    pairs = [(source, (source + steps) % count) for source in range(count)]
    return lax.ppermute(value, axis, pairs)


def after(value, *earlier):
    return lax.optimization_barrier((value, *earlier))[0]


def exact_pick(table, rows):
    return jnp.dot(table.astype(jnp.bfloat16), rows, preferred_element_type=jnp.float32)


def route_tables(route_ids, route_scores, flying):
    expert_ids = jnp.arange(flying, dtype=jnp.int32)
    matches = (route_ids[..., None] == expert_ids).astype(jnp.float32)
    hits = jnp.sum(matches, axis=3)
    weighted = (
        ROUTE_SCALE
        * jnp.sum(matches * route_scores[..., None], axis=3)
        / jnp.sum(route_scores, axis=3)[..., None]
    )
    places = jnp.cumsum(hits, axis=2) - 1.0
    slot_ids = jnp.arange(CAP, dtype=jnp.float32)
    placed = hits[..., None] * (places[..., None] == slot_ids).astype(jnp.float32)
    mixed = placed * weighted[..., None]
    earlier = jnp.cumsum(hits, axis=3) - hits
    firsts = placed * (earlier == 0.0).astype(jnp.float32)[..., None]
    flat = hits.shape[:3] + (flying * CAP,)
    return placed.reshape(flat), mixed.reshape(flat), firsts.reshape(flat)


def local(
    fwd_state,
    rev_state,
    norm_gain,
    w_gate,
    w_up,
    w_down,
    routes_fwd,
    scores_fwd,
    routes_rev,
    scores_rev,
):
    flying = lax.axis_size("g")
    pairs = lax.axis_size("h")
    width = fwd_state.shape[2]
    slots = flying * CAP
    gain_row = norm_gain[0]
    ways = (1, -1)

    def widened(block, axis):
        near = shifted(block, "b", 1)
        return jnp.concatenate(
            [block, shifted(block, "c", 1), near, shifted(near, "c", 1)], axis=axis
        )

    def exchange(blocks):
        return lax.all_to_all(blocks, ("g", "h"), split_axis=0, concat_axis=0, tiled=True)

    def spread(per_expert, stream):
        by_expert = per_expert.reshape(flying, CAP, -1)
        empty = jnp.zeros_like(by_expert)
        both = (by_expert, empty) if stream == 0 else (empty, by_expert)
        return jnp.concatenate(both, axis=1).reshape(2 * slots, -1)

    placed, mixed, firsts = route_tables(
        jnp.stack([routes_fwd[:, 0], routes_rev[:, 0]]),
        jnp.stack([scores_fwd[:, 0], scores_rev[:, 0]]),
        flying,
    )
    placed = placed.swapaxes(2, 3)
    mixing = jnp.einsum("stkr,strq->stkq", placed, mixed, precision=lax.Precision.HIGHEST)
    mixing = [
        [spread(mixing[s, t].T, s).T for t in range(STEPS)] for s in range(2)
    ]
    heard = [shifted(firsts[s].astype(jnp.bfloat16), "pipe", ways[s]) for s in range(2)]
    heard = [value.astype(jnp.float32) for value in heard]
    kept = [1.0 - jnp.sum(value, axis=2) for value in heard]

    def wanted_from(s, t):
        if t == 0:
            return placed[s, 0], None
        return placed[s, t] * kept[s][t - 1], placed[s, t] @ heard[s][t - 1]

    def gathered(rows, changed, from_rows, from_changed):
        found = exact_pick(from_rows, rows)
        if changed is not None:
            found = found + exact_pick(from_changed, changed)
        return found

    def merged_rows(rows, changed, s, t):
        return (
            kept[s][t][:, None] * rows.astype(jnp.float32) + exact_pick(heard[s][t], changed)
        ).astype(jnp.bfloat16)

    gate_cols = widened(w_gate[0], 1)
    up_cols = widened(w_up[0], 1)
    down_rows = widened(w_down[0], 0)

    rows = [fwd_state[0], rev_state[0]]
    base = rows
    changed = [None, None]
    for t in range(STEPS):
        tables = [wanted_from(s, t) for s in range(2)]
        found = sum(
            gathered(
                base[s],
                changed[s],
                spread(tables[s][0], s),
                None if changed[s] is None else spread(tables[s][1], s),
            )
            for s in range(2)
        )
        factor = lax.rsqrt(jnp.mean(found * found, axis=-1, keepdims=True) + EPSILON)
        normed = (found * factor * gain_row).astype(jnp.bfloat16)
        sent = jnp.broadcast_to(
            normed.reshape(flying, 1, 2 * CAP, width), (flying, pairs, 2 * CAP, width)
        ).reshape(flying * pairs, 2 * CAP, width)
        got = exchange(sent)

        if t > 0:
            rows = [merged_rows(base[s], after(changed[s], sent), s, t - 1) for s in range(2)]
        next_base = [shifted(rows[s], "pipe", ways[s]) for s in range(2)]
        own = [exact_pick(placed[s, t], rows[s]) for s in range(2)]

        tok_rows = after(got, *own).reshape(-1, width)
        gate_act = jnp.dot(tok_rows, gate_cols, preferred_element_type=jnp.float32)
        up_act = jnp.dot(tok_rows, up_cols, preferred_element_type=jnp.float32)
        hidden = (jax.nn.silu(gate_act) * up_act).astype(jnp.bfloat16)
        part = jnp.dot(hidden, down_rows, preferred_element_type=jnp.float32).astype(jnp.bfloat16)
        back = exchange(part.reshape(flying * pairs, 2 * CAP, width))

        summed = jnp.sum(
            back.astype(jnp.float32).reshape(flying, pairs, 2 * CAP, width), axis=1
        ).reshape(2 * slots, width)
        added = jnp.dot(
            jnp.concatenate([mixing[s][t] for s in range(2)]),
            summed,
            precision=lax.Precision.HIGHEST,
        )
        renewed = (jnp.concatenate(own) + added).astype(jnp.bfloat16)
        changed = [
            shifted(renewed[s * slots : (s + 1) * slots], "pipe", ways[s]) for s in range(2)
        ]
        base = next_base
    out = [merged_rows(base[s], changed[s], s, STEPS - 1) for s in range(2)]
    return (out[0][None], out[1][None])


def solution(mesh):
    pipe, expert = mesh.devices.shape
    devices = mesh.devices.reshape(pipe, GROUP, expert // (GROUP * PAIRS * 2), PAIRS, 2)
    split = Mesh(devices, ("pipe", "g", "h", "b", "c"))
    column = ("g", "h", "b", "c")
    in_specs = (
        P("pipe", column, None),
        P("pipe", column, None),
        P("pipe", None),
        P("pipe", None, column),
        P("pipe", None, column),
        P("pipe", column, None),
        P(None, "pipe", column, None),
        P(None, "pipe", column, None),
        P(None, "pipe", column, None),
        P(None, "pipe", column, None),
    )
    out_specs = (P("pipe", column, None), P("pipe", column, None))
    return jax.shard_map(local, mesh=split, in_specs=in_specs, out_specs=out_specs, check_vma=False)
```
